32 devices in a mesh: group: 2 (over y), row: 4 (over x, core), col: 4 (over z).
Axes of the slice: x: 2, y: 2, z: 4, core: 2. Of those that a mesh axis runs over, the one named last changes fastest.
Arguments:
- tokens: bfloat16 [1024, 8192], P(('group', 'col'), 'row'), parts along dimension 0, may hold values from -6 to 6
- gate_weight: bfloat16 [8192, 14336], P('row', 'col'), may hold values from -0.0625 to 0.0625
- up_weight: bfloat16 [8192, 14336], P('row', 'col'), may hold values from -0.0625 to 0.0625
Outputs:
- hessian: float32 [28672, 14336], P(('group', 'row'), 'col'), parts along dimension 0
The draws below stay inside these ranges and needn't reach their ends.
There are 2 independent parts, one for each index of `group`. The reference program is written for one: setup_inputs(seed, part) draws one part's arguments, and reference() takes and returns one part's arrays. A program takes and returns all parts, laid end to end along the dimension named above; an argument that names none is the same for every part. Nothing has to cross between parts.
All inputs are finite; a program needn't handle non-finite values.
Results may differ from the reference program's by a relative error of at most 0.0039.
Values may be sent and summed in bfloat16 or wider, within the bound.
No kernel may reach another device: no remote copies, remote signals or barrier semaphores. Data moves between devices by JAX's collectives and lax.ppermute only.
A program may use at most 128 MiB of HBM per device.

```python
import jax
import jax.numpy as jnp

D = 8192
UNITS = 14336
BLOCK = 1792
TOKENS = 512


def shard_levels(rng, dims, split, least, high):
    loudness, own = 1.0, jax.random.fold_in(rng, 6)
    for position, blocks in split:
        heights = jnp.exp(jax.random.uniform(jax.random.fold_in(own, position), (blocks,), jnp.float32, least / len(split), high / len(split)))
        loudness = loudness * jnp.repeat(heights, dims[position] // blocks).reshape([-1 if axis == position else 1 for axis in range(len(dims))])
    return loudness


def centred(stream_key, shape, spread, most, cuts=(), kind=jnp.bfloat16):
    loudness = shard_levels(stream_key, shape, cuts, -0.22, 0.18) if cuts else 1.0
    result = jax.random.normal(stream_key, shape, jnp.float32) * spread * loudness
    return jnp.minimum(jnp.maximum(result, -most), most).astype(kind)


def setup_inputs(seed: int = 0, part: int = 0) -> dict:
    seeds = jax.random.split(jax.random.key(seed), 4)
    part_keys = jax.random.split(jax.random.fold_in(seeds[3], part), 4)
    return {
        "tokens": centred(part_keys[0], (TOKENS, D), 1.0, 6.0, ((0, 4), (1, 4))),
        "gate_weight": centred(seeds[1], (D, UNITS), D ** -0.5, 0.0625, ((0, 4), (1, 4))),
        "up_weight": centred(seeds[2], (D, UNITS), D ** -0.5, 0.0625, ((0, 4), (1, 4))),
    }


def reference(tokens, gate_weight, up_weight):
    gate_values = jnp.dot(tokens, gate_weight, preferred_element_type=jnp.float32)
    up_values = jnp.dot(tokens, up_weight, preferred_element_type=jnp.float32)
    hidden = (jax.nn.silu(gate_values) * up_values).astype(jnp.bfloat16)
    gram = jnp.dot(hidden.T, hidden, preferred_element_type=jnp.float32) * (2.0 / TOKENS)
    blocks = jnp.arange(UNITS, dtype=jnp.int32) // BLOCK
    upper_mask = blocks[:, None] <= blocks[None, :]
    return jnp.where(upper_mask, gram, jnp.zeros_like(gram))
```

```python
import functools
import math

import jax
import jax.numpy as jnp
from jax import lax
from jax.experimental import pallas as pl
from jax.experimental.pallas import tpu as pltpu
from jax.sharding import PartitionSpec as P

BLOCK = 1792
TOKEN_MAX = 6.0
WEIGHT_MAX = 0.0625
PAIR = 2
UNIT_PARTS = 2


def send_scale(features):
    bound = TOKEN_MAX * WEIGHT_MAX * features
    return 2.0 ** math.floor(math.log2(float(jnp.finfo(jnp.float16).max) / bound))


def divisor(limit, *sizes):
    return max(d for d in range(128, limit + 1, 128) if all(s % d == 0 for s in sizes))


def project(sources, shards, gate, up, part, parts, row_index, col_index, rows):
    shard_rows, features = sources[0].shape
    width = gate.shape[1] // parts
    tokens = len(shards) * shard_rows
    piece = tokens // rows
    chips = rows // PAIR
    half = tokens // PAIR
    per_shard = shard_rows // piece
    tile = divisor(256, width)
    steps = width // tile
    distances = sorted(sources)

    def kernel(meta, *refs):
        source_refs = dict(zip(distances, refs[: len(distances)]))
        gate_ref, up_ref, keep_ref, send_ref, held, sems = refs[len(distances):]

        @pl.when(pl.program_id(0) == 0)
        def _():
            chip, core, col = meta[0] // PAIR, meta[0] % PAIR, meta[1]
            waits = []
            for place, shard in enumerate(shards):
                for b in range(per_shard):
                    q = place * per_shard + b
                    step = lax.rem(q // PAIR - chip + chips, chips)
                    role = jnp.where(core == q % PAIR, 0, chips) + step
                    target = held.at[pl.ds(pl.multiple_of(role * piece, piece), piece)]
                    for d in distances:
                        if 0 <= shard - d:
                            copy = pltpu.make_async_copy(
                                source_refs[d].at[pl.ds(b * piece, piece)], target, sems.at[q]
                            )
                            pl.when(col == shard - d)(copy.start)
                    waits.append(
                        pltpu.make_async_copy(
                            source_refs[0].at[pl.ds(b * piece, piece)], target, sems.at[q]
                        )
                    )
            for wait in waits:
                wait.wait()

        for index, weight in enumerate((gate_ref, up_ref)):
            result = jnp.dot(held[...], weight[...], preferred_element_type=jnp.float32)
            keep_ref[index] = result[:half]
            send_ref[index] = result[half:]

    weight_spec = pl.BlockSpec((features, tile), lambda j, meta: (0, part * steps + j))
    out_spec = pl.BlockSpec((2, half, tile), lambda j, meta: (0, 0, j))
    return pl.pallas_call(
        kernel,
        grid_spec=pltpu.PrefetchScalarGridSpec(
            num_scalar_prefetch=1,
            grid=(steps,),
            in_specs=[pl.BlockSpec(memory_space=pl.ANY)] * len(distances)
            + [weight_spec, weight_spec],
            out_specs=[out_spec, out_spec],
            scratch_shapes=[
                pltpu.VMEM((tokens, features), sources[0].dtype),
                pltpu.SemaphoreType.DMA((rows,)),
            ],
        ),
        out_shape=[
            jax.ShapeDtypeStruct((2, half, width), jnp.float32),
            jax.ShapeDtypeStruct((2, half, width), jnp.float32),
        ],
        cost_estimate=pl.CostEstimate(
            flops=4 * tokens * features * width,
            bytes_accessed=4 * features * width + 12 * half * width,
            transcendentals=0,
        ),
        name=f"project_{shards[0]}_{part}",
    )(jnp.stack([row_index, col_index]), *[sources[d] for d in distances], gate, up)


def gram_block(row_pieces, col_pieces, out, place, shape, row_base, col_base, factor):
    m, n = row_pieces[0].shape[1], col_pieces[0].shape[1]
    tile_m = divisor(896, m, BLOCK)
    tile_n = divisor(896, n, BLOCK)
    count = len(row_pieces)

    def kernel(meta, *refs):
        row_refs, col_refs, out_ref = refs[:count], refs[count : 2 * count], refs[-1]
        i, j = pl.program_id(0), pl.program_id(1)
        row_block = (meta[0] + i * tile_m) // BLOCK
        col_block = (meta[1] + j * tile_n) // BLOCK

        @pl.when(row_block <= col_block)
        def _():
            total = None
            for a, b in zip(row_refs, col_refs):
                term = lax.dot_general(
                    a[...], b[...], (((0,), (0,)), ((), ())), preferred_element_type=jnp.float32
                )
                total = term if total is None else total + term
            out_ref[...] = total * factor

        @pl.when(row_block > col_block)
        def _():
            out_ref[...] = jnp.zeros_like(out_ref)

    in_specs = [pl.BlockSpec((p.shape[0], tile_m), lambda i, j, meta: (0, i)) for p in row_pieces]
    in_specs += [pl.BlockSpec((p.shape[0], tile_n), lambda i, j, meta: (0, j)) for p in col_pieces]
    args = [*row_pieces, *col_pieces]
    aliases = {}
    if out is not None:
        in_specs.append(pl.BlockSpec(memory_space=pl.ANY))
        aliases = {1 + len(args): 0}
        args.append(out)
    i0, j0 = place[0] // tile_m, place[1] // tile_n
    tokens = sum(p.shape[0] for p in row_pieces)
    return pl.pallas_call(
        kernel,
        grid_spec=pltpu.PrefetchScalarGridSpec(
            num_scalar_prefetch=1,
            grid=(m // tile_m, n // tile_n),
            in_specs=in_specs,
            out_specs=pl.BlockSpec((tile_m, tile_n), lambda i, j, meta: (i0 + i, j0 + j)),
        ),
        out_shape=jax.ShapeDtypeStruct(shape, jnp.float32),
        input_output_aliases=aliases,
        cost_estimate=pl.CostEstimate(
            flops=2 * tokens * m * n, bytes_accessed=4 * m * n, transcendentals=0
        ),
        name=f"gram_{place[0]}_{place[1]}",
    )(jnp.stack([row_base, col_base]), *args)


def body(tokens, gate_weight, up_weight):
    rows = lax.axis_size("row")
    cols = lax.axis_size("col")
    row_index = lax.axis_index("row").astype(jnp.int32)
    col_index = lax.axis_index("col").astype(jnp.int32)
    chips = rows // PAIR
    width = gate_weight.shape[1]
    token_count = tokens.shape[0] * cols
    per_column = rows // cols
    own_units = width // per_column
    parts = UNIT_PARTS
    part_width = width // parts
    scale = send_scale(tokens.shape[1] * PAIR)

    partner = [(r, r ^ 1) for r in range(rows)]

    def chip_shift(s):
        return [(r, (r + s * PAIR) % rows) for r in range(rows)]

    sources = {0: tokens}
    right = left = tokens
    for d in range(1, cols):
        right = lax.ppermute(right, "col", [(c, c + 1) for c in range(d - 1, cols - 1)])
        left = lax.ppermute(left, "col", [(c, c - 1) for c in range(1, cols - d + 1)])
        sources[-d], sources[d] = right, left

    quarter = cols // 4
    inner = list(range(quarter, cols - quarter))
    outer = [c for c in range(cols) if c not in inner]
    subsets = (inner, outer)

    hidden = {}
    for which, shards in enumerate(subsets):
        reach = max(max(abs(s - c) for s in shards) for c in range(cols))
        near = {d: v for d, v in sources.items() if abs(d) <= reach}
        for part in range(parts):
            keep, send = project(
                near, shards, gate_weight, up_weight, part, parts, row_index, col_index, rows
            )
            piece = keep.shape[1] // chips
            other = lax.ppermute(send, "row", partner)
            added = [
                keep[:, s * piece : (s + 1) * piece]
                + other[:, s * piece : (s + 1) * piece]
                for s in range(chips)
            ]
            values = added[0]
            for s in range(1, chips):
                got = lax.ppermute((added[s] * scale).astype(jnp.float16), "row", chip_shift(s))
                values = values + got.astype(jnp.float32) * (1 / scale)
            own = (jax.nn.silu(values[0]) * values[1]).astype(jnp.bfloat16)
            mine = [own] + [lax.ppermute(own, "row", chip_shift(s)) for s in range(1, chips)]
            mine = jnp.concatenate(mine, axis=0)
            theirs = lax.ppermute(mine, "row", partner)
            hidden[which, part] = jnp.concatenate([mine, theirs], axis=0)

    def spread(value):
        result = None
        moving = value
        for hop in range(1, cols):
            pairs = [
                (r * cols + r // per_column + hop - 1, r * cols + r // per_column + hop)
                for r in range(rows)
                if r // per_column + hop < cols
            ]
            if not pairs:
                break
            moving = lax.ppermute(moving, ("row", "col"), pairs)
            result = moving if result is None else result + moving
        here = col_index == row_index // per_column
        return value if result is None else jnp.where(here, value, result)

    row_side = {}
    row_parts = parts if per_column == 1 else 1
    for which in range(len(subsets)):
        if per_column == 1:
            for part in range(parts):
                row_side[which, part] = spread(hidden[which, part])
        else:
            joined = jnp.concatenate([hidden[which, p] for p in range(parts)], axis=1)
            offset = row_index % per_column * own_units
            row_side[which, 0] = spread(lax.dynamic_slice_in_dim(joined, offset, own_units, 1))

    out = None
    row_width = own_units // row_parts
    for a in range(row_parts):
        for b in range(parts):
            out = gram_block(
                [row_side[which, a] for which in range(len(subsets))],
                [hidden[which, b] for which in range(len(subsets))],
                out,
                (a * row_width, b * part_width),
                (own_units, width),
                row_index * own_units + a * row_width,
                col_index * width + b * part_width,
                2.0 / token_count,
            )
    return out


def solution(mesh):
    return jax.shard_map(
        body,
        mesh=mesh,
        in_specs=(P(("group", "col"), "row"), P("row", "col"), P("row", "col")),
        out_specs=P(("group", "row"), "col"),
        check_vma=False,
    )
```

```python
import math

import jax
import jax.numpy as jnp
from jax import lax
from jax.experimental import pallas as pl
from jax.experimental.pallas import tpu as pltpu
from jax.sharding import PartitionSpec as P

BLOCK = 1792
TOKEN_MAX = 6.0
WEIGHT_MAX = 0.0625
PAIR = 2
PARTS = 2
MIN_ROWS = 16


def send_scale(features):
    bound = TOKEN_MAX * WEIGHT_MAX * features
    return 2.0 ** math.floor(math.log2(float(jnp.finfo(jnp.float16).max) / bound))


def divisor(limit, *sizes):
    return max(d for d in range(128, limit + 1, 128) if all(s % d == 0 for s in sizes))


def arrival_order(cols, span):
    def distance(c, g):
        return max(abs(g * span + i - c) for i in range(span))

    return [
        sorted(range(cols // span), key=lambda g: (distance(c, g), abs(2 * g * span - cols)))
        for c in range(cols)
    ]


def project(sources, order, meta, gate, up, chunk, span, rows):
    turns, offset, width = chunk
    cols, groups = len(order), len(order[0])
    shard_rows, features = sources[0].shape
    options = [
        sorted({order[c][k] * span + i - c for c in range(cols)}) for k in turns for i in range(span)
    ]
    used = sorted(set().union(*options))
    tokens = len(options) * shard_rows
    piece = tokens // rows
    chips = rows // PAIR
    half = tokens // PAIR
    per_shard = shard_rows // piece
    tile = divisor(1792, width, offset) if offset else divisor(1792, width)
    steps, first = width // tile, offset // tile

    def kernel(meta, *refs):
        source_refs = dict(zip(used, refs[: len(used)]))
        gate_ref, up_ref, keep_ref, send_ref, held, sems = refs[len(used):]

        @pl.when(pl.program_id(0) == 0)
        def _():
            chip, core, col = meta[0] // PAIR, lax.rem(meta[0], PAIR), meta[1]
            waits = []
            for i, distances in enumerate(options):
                group = meta[2 + col * groups + turns[i // span]]
                here = group * span + i % span - col
                for b in range(per_shard):
                    q = i * per_shard + b
                    step = lax.rem(q // PAIR - chip + chips, chips)
                    role = jnp.where(core == q % PAIR, 0, chips) + step
                    target = held.at[pl.ds(pl.multiple_of(role * piece, piece), piece)]
                    for d in distances:
                        copy = pltpu.make_async_copy(
                            source_refs[d].at[pl.ds(b * piece, piece)], target, sems.at[q]
                        )
                        pl.when(here == d)(copy.start)
                    waits.append(
                        pltpu.make_async_copy(
                            source_refs[distances[0]].at[pl.ds(b * piece, piece)], target, sems.at[q]
                        )
                    )
            for wait in waits:
                wait.wait()

        for index, weight in enumerate((gate_ref, up_ref)):
            result = jnp.dot(held[...], weight[...], preferred_element_type=jnp.float32)
            keep_ref[index] = result[:half]
            send_ref[index] = result[half:]

    weight_spec = pl.BlockSpec((features, tile), lambda j, meta: (0, first + j))
    out_spec = pl.BlockSpec((2, half, tile), lambda j, meta: (0, 0, j))
    return pl.pallas_call(
        kernel,
        grid_spec=pltpu.PrefetchScalarGridSpec(
            num_scalar_prefetch=1,
            grid=(steps,),
            in_specs=[pl.BlockSpec(memory_space=pl.ANY)] * len(used) + [weight_spec, weight_spec],
            out_specs=[out_spec, out_spec],
            scratch_shapes=[
                pltpu.VMEM((tokens, features), sources[0].dtype),
                pltpu.SemaphoreType.DMA((rows,)),
            ],
        ),
        out_shape=[jax.ShapeDtypeStruct((2, half, width), jnp.float32)] * 2,
        cost_estimate=pl.CostEstimate(
            flops=4 * tokens * features * width,
            bytes_accessed=4 * features * width + 16 * half * width,
            transcendentals=0,
        ),
        name=f"project_{turns[0]}_{offset}",
    )(meta, *[sources[d] for d in used], gate, up)


def gram_rows(row_pieces, col_pieces, out, start, height, shape, meta, groups, group_rows, rows, per_column, lane):
    width = shape[1]
    tile = divisor(256, height, start, BLOCK) if start else divisor(256, height, BLOCK)
    segment = divisor(1792, width, BLOCK)
    tokens = groups * group_rows
    chips = rows // PAIR
    cols = rows // per_column
    arrays = []

    def index_of(array):
        for i, other in enumerate(arrays):
            if other is array:
                return i
        arrays.append(array)
        return len(arrays) - 1

    plan = []
    for side, pieces in enumerate((row_pieces, col_pieces)):
        for choices, turns, source_column, columns, column in pieces:
            indexed = [(index_of(a), *rest) for a, *rest in choices]
            plan += [(side, indexed, turns, b, source_column, columns, column) for b in range(rows)]

    def kernel(meta, *refs):
        array_refs = refs[: len(arrays)]
        out_ref, row_held, col_held, sems = refs[-4:]
        row, col = meta[0], meta[1]
        chip, core, source = row // PAIR, lax.rem(row, PAIR), row // per_column
        hop = col - source

        @pl.when(pl.program_id(0) == 0)
        def _():
            waits = []
            for n, (side, choices, turns, b, source_column, columns, column) in enumerate(plan):
                piece = len(turns) * group_rows // rows
                held = (row_held, col_held)[side]
                for index, distance, other_lane, ahead in choices:
                    chip_b = lax.rem(chip + ahead - b % chips + chips, chips)
                    core_b = lax.rem(core + b // chips, PAIR)
                    place = (chip_b * PAIR + core_b) * piece
                    slot = turns[0] + place // group_rows
                    position = meta[2 + (source if side == 0 else col) * groups + slot]
                    target_row = position * group_rows + lax.rem(place, group_rows)
                    copy = pltpu.make_async_copy(
                        array_refs[index].at[pl.ds(b * piece, piece), pl.ds(source_column, columns)],
                        held.at[
                            pl.ds(pl.multiple_of(target_row, piece), piece), pl.ds(column, columns)
                        ],
                        sems.at[n],
                    )
                    chosen = jnp.bool_(True)
                    if distance is not None:
                        chosen = jnp.maximum(hop, 0) == distance
                    if other_lane is not None:
                        chosen = chosen & ((source < lane) == other_lane)
                    pl.when(chosen)(copy.start)
                waits.append(copy)
            for wait in waits:
                wait.wait()

        own_units = shape[0]
        i = pl.program_id(0)
        row_block = (row * own_units + start + i * tile) // BLOCK
        for j in range(0, width, segment):
            col_block = (col * width + j) // BLOCK

            @pl.when(row_block <= col_block)
            def _():
                a = row_held[:, pl.ds(pl.multiple_of(i * tile, tile), tile)]
                total = lax.dot_general(
                    a,
                    col_held[:, j : j + segment],
                    (((0,), (0,)), ((), ())),
                    preferred_element_type=jnp.float32,
                )
                out_ref[:, j : j + segment] = total * (2.0 / tokens)

            @pl.when(row_block > col_block)
            def _():
                out_ref[:, j : j + segment] = jnp.zeros((tile, segment), jnp.float32)

    in_specs = [pl.BlockSpec(memory_space=pl.ANY)] * len(arrays)
    args = list(arrays)
    aliases = {}
    if out is not None:
        in_specs.append(pl.BlockSpec(memory_space=pl.ANY))
        aliases = {1 + len(args): 0}
        args.append(out)
    first = start // tile
    dtype = arrays[0].dtype
    return pl.pallas_call(
        kernel,
        grid_spec=pltpu.PrefetchScalarGridSpec(
            num_scalar_prefetch=1,
            grid=(height // tile,),
            in_specs=in_specs,
            out_specs=pl.BlockSpec((tile, width), lambda i, meta: (first + i, 0)),
            scratch_shapes=[
                pltpu.VMEM((tokens, height), dtype),
                pltpu.VMEM((tokens, width), dtype),
                pltpu.SemaphoreType.DMA((len(plan),)),
            ],
        ),
        out_shape=jax.ShapeDtypeStruct(shape, jnp.float32),
        input_output_aliases=aliases,
        cost_estimate=pl.CostEstimate(
            flops=2 * tokens * height * width, bytes_accessed=4 * height * width, transcendentals=0
        ),
        name=f"gram_{start}",
    )(meta, *args)


def body(tokens, gate_weight, up_weight):
    rows = lax.axis_size("row")
    cols = lax.axis_size("col")
    chips = rows // PAIR
    shard_rows, features = tokens.shape
    width = gate_weight.shape[1]
    per_column = rows // cols
    own_units = width // per_column
    span = max(1, MIN_ROWS * rows // shard_rows)
    groups = cols // span
    order = arrival_order(cols, span)
    scale = send_scale(features * PAIR)
    lane = cols // 2
    ahead = chips // 2

    here = jnp.stack([lax.axis_index("row"), lax.axis_index("col")]).astype(jnp.int32)
    table = jnp.array([g for c in order for g in c], jnp.int32)
    meta = jnp.concatenate([here, table])

    partner = [(r, r ^ 1) for r in range(rows)]

    def chip_shift(s):
        return [(r, (r + s * PAIR) % rows) for r in range(rows)]

    sources = {0: tokens}
    right = left = tokens
    for d in range(1, cols):
        right = lax.ppermute(right, "col", [(c, c + 1) for c in range(d - 1, cols - 1)])
        left = lax.ppermute(left, "col", [(c, c - 1) for c in range(1, cols - d + 1)])
        sources[-d], sources[d] = right, left

    part_width = width // PARTS
    chunks = [([k], 0, width) for k in range(groups - 2)]
    chunks += [([groups - 2, groups - 1], p * part_width, part_width) for p in range(PARTS)]

    hidden = []
    for chunk in chunks:
        keep, send = project(sources, order, meta, gate_weight, up_weight, chunk, span, rows)
        piece = keep.shape[1] // chips
        other = lax.ppermute(send, "row", partner)
        added = [
            keep[:, s * piece : (s + 1) * piece] + other[:, s * piece : (s + 1) * piece]
            for s in range(chips)
        ]
        values = added[0]
        for s in range(1, chips):
            got = lax.ppermute((added[s] * scale).astype(jnp.float16), "row", chip_shift(s))
            values = values + got.astype(jnp.float32) * (1 / scale)
        own = (jax.nn.silu(values[0]) * values[1]).astype(jnp.bfloat16)
        mine = [own] + [lax.ppermute(own, "row", chip_shift(s)) for s in range(1, chips)]
        mine = jnp.concatenate(mine, axis=0)
        theirs = lax.ppermute(mine, "row", partner)
        hidden.append(jnp.concatenate([mine, theirs], axis=0))

    def travel(value, lines):
        result = []
        for hop in range(1, cols):
            pairs = [
                (at * cols + r // per_column + hop - 1, at * cols + r // per_column + hop)
                for r, at in lines
                if r // per_column + hop < cols
            ]
            if not pairs:
                break
            value = lax.ppermute(value, ("row", "col"), pairs)
            result.append((value, [(a // cols, a % cols) for _, a in pairs]))
        return result

    def row_choices(value, split):
        direct = [(r, r) for r in range(rows) if not (split and r // per_column < lane)]
        choices = [(value, 0, None, 0)]
        kind = False if split else None
        for hop, (moved, _) in enumerate(travel(value, direct), 1):
            choices.append((moved, hop, kind, 0))
        if split:
            lines = [
                (r, (r + ahead * PAIR) % rows) for r in range(rows) if r // per_column < lane
            ]
            for hop, (moved, ends) in enumerate(travel(value, lines), 1):
                back = [(a * cols + c, (a - ahead * PAIR) % rows * cols + c) for a, c in ends]
                moved = lax.ppermute(moved, ("row", "col"), back)
                choices.append((moved, hop, True, ahead))
        return choices

    can_split = ahead > 0 and ahead * PAIR % per_column == 0 and groups > 3
    split_chunk = 1 if can_split else None
    row_side = []
    if per_column == 1:
        for i, (turns, offset, columns) in enumerate(chunks):
            row_side.append((row_choices(hidden[i], i == split_chunk), turns, offset, columns))
        heights = [(p * part_width, part_width) for p in range(PARTS)]
    else:
        offset = lax.rem(here[0], jnp.int32(per_column)) * own_units
        joined = hidden[: groups - 2] + [jnp.concatenate(hidden[groups - 2 :], axis=1)]
        for i, value in enumerate(joined):
            value = lax.dynamic_slice_in_dim(value, offset, own_units, 1)
            row_side.append((row_choices(value, i == split_chunk), chunks[i][0], 0, own_units))
        heights = [(0, own_units)]

    col_pieces = [
        ([(hidden[i], None, None, 0)], turns, 0, columns, offset)
        for i, (turns, offset, columns) in enumerate(chunks)
    ]
    out = None
    for start, height in heights:
        row_pieces = [
            (choices, turns, start - offset, height, 0)
            for choices, turns, offset, columns in row_side
            if offset <= start and start + height <= offset + columns
        ]
        out = gram_rows(
            row_pieces, col_pieces, out, start, height, (own_units, width), meta,
            groups, span * shard_rows, rows, per_column, lane,
        )
    return out


def solution(mesh):
    return jax.shard_map(
        body,
        mesh=mesh,
        in_specs=(P(("group", "col"), "row"), P("row", "col"), P("row", "col")),
        out_specs=P(("group", "row"), "col"),
        check_vma=False,
    )
```

```python
import math

import jax
import jax.numpy as jnp
from jax import lax
from jax.experimental import pallas as pl
from jax.experimental.pallas import tpu as pltpu
from jax.sharding import PartitionSpec as P


BLOCK = 1792
TOKEN_MAX = 6.0
WEIGHT_MAX = 0.0625
PAIR = 2
PARTS = 2
MIN_ROWS = 16
AHEAD = 2
PROJECT_VMEM = 18 * 2**20
GRAM_VMEM = 24 * 2**20


def send_scale(features):
    bound = TOKEN_MAX * WEIGHT_MAX * features
    return 2.0 ** math.floor(math.log2(float(jnp.finfo(jnp.float16).max) / bound))


def in_hbm(array):
    return pltpu.with_memory_space_constraint(array, pltpu.HBM)


def holds(column, kind, number):
    if kind == "parity":
        return column % 2 == number
    return column < number if kind == "below" else column >= number


def divisor(limit, *sizes):
    return max(d for d in range(128, limit + 1, 128) if all(s % d == 0 for s in sizes))


def arrival_order(cols, span):
    def distance(c, g):
        return max(abs(g * span + i - c) for i in range(span))

    return [
        sorted(range(cols // span), key=lambda g: (distance(c, g), abs(2 * g * span - cols)))
        for c in range(cols)
    ]


def project(sources, order, meta, weights, chunk, span, rows, mode):
    turns, offset, width = chunk
    count = len(weights)
    cols, groups = len(order), len(order[0])
    shard_rows, features = sources[0].shape
    options = [
        sorted({order[c][k] * span + i - c for c in range(cols)}) for k in turns for i in range(span)
    ]
    used = sorted(set().union(*options))
    tokens = len(options) * shard_rows
    piece = tokens // rows
    chips = rows // PAIR
    half = tokens // PAIR
    per_shard = shard_rows // piece
    tile = divisor(512, width) if width % 512 == 0 else divisor(896, width)
    steps = width // tile

    def kernel(meta, *refs):
        source_refs = dict(zip(used, refs[: len(used)]))
        given, keep_ref, send_ref = refs[len(used) :][:count], *refs[len(used) + count :][:2]
        start = offset
        if mode == "load":
            weight_refs = refs[len(used) + count + 2 :][:count]
            held, sems, load_sems = refs[-3:]
        elif mode == "stream":
            held, sems, load_sems, stream = refs[-4:]
            weight_refs = [stream.at[n] for n in range(count)]
            start = 0
        else:
            weight_refs = given
            held, sems = refs[-2:]

        def load_copy(index, j):
            block = pl.ds(pl.multiple_of(offset + j * tile, 128), tile)
            place = pl.ds(pl.multiple_of(start + j * tile, 128), tile)
            source, target = given[index].at[:, block], weight_refs[index].at[:, place]
            return pltpu.make_async_copy(source, target, load_sems.at[index, j])

        @pl.when(pl.program_id(0) == 0)
        def _():
            chip, core, col = meta[0] // PAIR, lax.rem(meta[0], PAIR), meta[1]
            waits = []
            for i, distances in enumerate(options):
                group = meta[2 + col * groups + turns[i // span]]
                away = group * span + i % span - col
                for b in range(per_shard):
                    q = i * per_shard + b
                    step = lax.rem(q // PAIR - chip + chips, chips)
                    role = jnp.where(core == q % PAIR, 0, chips) + step
                    target = held.at[pl.ds(pl.multiple_of(role * piece, piece), piece)]
                    for d in distances:
                        copy = pltpu.make_async_copy(
                            source_refs[d].at[pl.ds(b * piece, piece)], target, sems.at[q]
                        )
                        pl.when(away == d)(copy.start)
                    waits.append(
                        pltpu.make_async_copy(
                            source_refs[distances[0]].at[pl.ds(b * piece, piece)], target, sems.at[q]
                        )
                    )
            if mode != "held":
                for j in range(min(AHEAD, steps)):
                    for index in range(count):
                        load_copy(index, j).start()
            for wait in waits:
                wait.wait()

        if mode != "held":

            @pl.when(pl.program_id(0) + AHEAD < steps)
            def _():
                for index in range(count):
                    load_copy(index, pl.program_id(0) + AHEAD).start()

        here = pl.ds(pl.multiple_of(start + pl.program_id(0) * tile, 128), tile)
        for index, weight in enumerate(weight_refs):
            if mode != "held":
                load_copy(index, pl.program_id(0)).wait()
            result = jnp.dot(held[...], weight[:, here], preferred_element_type=jnp.float32)
            keep_ref[index] = result[:half]
            send_ref[index] = result[half:]

    vmem_spec = pl.BlockSpec(memory_space=pltpu.VMEM)
    hbm_spec = pl.BlockSpec(memory_space=pltpu.HBM)
    weight_spec = vmem_spec if mode == "held" else hbm_spec
    out_spec = pl.BlockSpec((count, half, tile), lambda j, meta: (0, 0, j))
    return pl.pallas_call(
        kernel,
        grid_spec=pltpu.PrefetchScalarGridSpec(
            num_scalar_prefetch=1,
            grid=(steps,),
            in_specs=[hbm_spec] * len(used) + [weight_spec] * count,
            out_specs=[out_spec] * 2 + [vmem_spec] * (count if mode == "load" else 0),
            scratch_shapes=[
                pltpu.VMEM((tokens, features), sources[0].dtype),
                pltpu.SemaphoreType.DMA((rows,)),
            ]
            + ([] if mode == "held" else [pltpu.SemaphoreType.DMA((count, steps))])
            + ([pltpu.VMEM((count, features, width), weights[0].dtype)] if mode == "stream" else []),
        ),
        out_shape=[pltpu.HBM((count, half, width), jnp.float32)] * 2
        + ([pltpu.VMEM(w.shape, w.dtype) for w in weights] if mode == "load" else []),
        cost_estimate=pl.CostEstimate(
            flops=2 * count * tokens * features * width,
            bytes_accessed=2 * count * (features + 4 * half) * width,
            transcendentals=0,
        ),
        compiler_params=pltpu.CompilerParams(vmem_limit_bytes=PROJECT_VMEM),
    )(meta, *[in_hbm(sources[d]) for d in used], *(weights if mode == "held" else map(in_hbm, weights)))


def placed(pieces, groups, group_rows, rows, per_column, of_row):
    chips = rows // PAIR
    arrays = []

    def index_of(array):
        for i, other in enumerate(arrays):
            if other is array:
                return i
        arrays.append(array)
        return len(arrays) - 1

    plan = []
    for choices, turns, source_column, columns, column in pieces:
        indexed = [(index_of(a), *rest) for a, *rest in choices]
        plan += [(indexed, turns, b, source_column, columns, column) for b in range(rows)]

    def run(meta, array_refs, held, sems):
        row, col = meta[0], meta[1]
        chip, core, source = row // PAIR, lax.rem(row, PAIR), row // per_column
        hop = col - source
        waits = []
        for n, (choices, turns, b, source_column, columns, column) in enumerate(plan):
            piece = len(turns) * group_rows // rows
            for index, distance, sources, ahead in choices:
                chip_b = lax.rem(chip + ahead - b % chips + chips, chips)
                core_b = lax.rem(core + b // chips, PAIR)
                place = (chip_b * PAIR + core_b) * piece
                slot = turns[0] + place // group_rows
                position = meta[2 + (source if of_row else col) * groups + slot]
                target_row = position * group_rows + lax.rem(place, group_rows)
                copy = pltpu.make_async_copy(
                    array_refs[index].at[pl.ds(b * piece, piece), pl.ds(source_column, columns)],
                    held.at[pl.ds(pl.multiple_of(target_row, piece), piece), pl.ds(column, columns)],
                    sems.at[n],
                )
                chosen = jnp.bool_(True)
                if distance is not None:
                    chosen = jnp.maximum(hop, 0) == distance
                for condition in sources:
                    chosen = chosen & holds(source, *condition)
                pl.when(chosen)(copy.start)
            waits.append(copy)
        for wait in waits:
            wait.wait()

    return arrays, len(plan), run


def collect(pieces, shape, meta, groups, group_rows, rows, per_column):
    arrays, copies, run = placed(pieces, groups, group_rows, rows, per_column, False)

    def kernel(meta, *refs):
        run(meta, refs[: len(arrays)], refs[-2], refs[-1])

    return pl.pallas_call(
        kernel,
        grid_spec=pltpu.PrefetchScalarGridSpec(
            num_scalar_prefetch=1,
            grid=(1,),
            in_specs=[pl.BlockSpec(memory_space=pl.ANY)] * len(arrays),
            out_specs=pl.BlockSpec(memory_space=pltpu.VMEM),
            scratch_shapes=[pltpu.SemaphoreType.DMA((copies,))],
        ),
        out_shape=pltpu.VMEM(shape, arrays[0].dtype),
        compiler_params=pltpu.CompilerParams(vmem_limit_bytes=GRAM_VMEM),
        name="collect",
    )(meta, *arrays)


def gram_rows(row_pieces, columns, out, start, height, shape, meta, groups, group_rows, rows, per_column):
    width = shape[1]
    tile = divisor(256, height, start, BLOCK) if start else divisor(256, height, BLOCK)
    segment = divisor(1792, width, BLOCK)
    tokens = groups * group_rows
    arrays, copies, run = placed(row_pieces, groups, group_rows, rows, per_column, True)

    def kernel(meta, *refs):
        columns_ref = refs[len(arrays)]
        out_ref, row_held, sems = refs[-3:]
        row, col = meta[0], meta[1]

        @pl.when(pl.program_id(0) == 0)
        def _():
            run(meta, refs[: len(arrays)], row_held, sems)

        own_units = shape[0]
        i = pl.program_id(0)
        row_block = (row * own_units + start + i * tile) // BLOCK
        for j in range(0, width, segment):
            col_block = (col * width + j) // BLOCK

            @pl.when(row_block <= col_block)
            def _():
                a = row_held[:, pl.ds(pl.multiple_of(i * tile, tile), tile)]
                total = lax.dot_general(
                    a,
                    columns_ref[:, j : j + segment],
                    (((0,), (0,)), ((), ())),
                    preferred_element_type=jnp.float32,
                )
                out_ref[:, j : j + segment] = total * (2.0 / tokens)

            @pl.when(row_block > col_block)
            def _():
                out_ref[:, j : j + segment] = jnp.zeros((tile, segment), jnp.float32)

    in_specs = [pl.BlockSpec(memory_space=pl.ANY)] * len(arrays)
    in_specs.append(pl.BlockSpec(memory_space=pltpu.VMEM))
    args = [*arrays, columns]
    aliases = {}
    if out is not None:
        in_specs.append(pl.BlockSpec(memory_space=pl.ANY))
        aliases = {1 + len(args): 0}
        args.append(out)
    first = start // tile
    return pl.pallas_call(
        kernel,
        grid_spec=pltpu.PrefetchScalarGridSpec(
            num_scalar_prefetch=1,
            grid=(height // tile,),
            in_specs=in_specs,
            out_specs=pl.BlockSpec((tile, width), lambda i, meta: (first + i, 0)),
            scratch_shapes=[
                pltpu.VMEM((tokens, height), columns.dtype),
                pltpu.SemaphoreType.DMA((copies,)),
            ],
        ),
        out_shape=jax.ShapeDtypeStruct(shape, jnp.float32),
        input_output_aliases=aliases,
        cost_estimate=pl.CostEstimate(
            flops=2 * tokens * height * width, bytes_accessed=4 * height * width, transcendentals=0
        ),
        compiler_params=pltpu.CompilerParams(vmem_limit_bytes=GRAM_VMEM),
    )(meta, *args)


def body(tokens, gate_weight, up_weight):
    rows = lax.axis_size("row")
    cols = lax.axis_size("col")
    chips = rows // PAIR
    shard_rows, features = tokens.shape
    width = gate_weight.shape[1]
    per_column = rows // cols
    own_units = width // per_column
    span = max(1, MIN_ROWS * rows // shard_rows)
    groups = cols // span
    order = arrival_order(cols, span)
    scale = send_scale(features * PAIR)
    lane = cols // 2
    ahead = chips // 2

    here = jnp.stack([lax.axis_index("row"), lax.axis_index("col")]).astype(jnp.int32)
    table = jnp.array([g for c in order for g in c], jnp.int32)
    meta = jnp.concatenate([here, table])

    partner = [(r, r ^ 1) for r in range(rows)]

    def chip_shift(s):
        return [(r, (r + s * PAIR) % rows) for r in range(rows)]

    sources = {0: tokens}
    right = left = tokens
    for d in range(1, cols):
        right = lax.ppermute(right, "col", [(c, c + 1) for c in range(d - 1, cols - 1)])
        left = lax.ppermute(left, "col", [(c, c - 1) for c in range(1, cols - d + 1)])
        sources[-d], sources[d] = right, left

    part_width = width // PARTS
    chunks = [([k], 0, width) for k in range(groups - 2)]
    chunks += [([groups - 2, groups - 1], p * part_width, part_width) for p in range(PARTS)]

    hidden = []
    held = []
    for i, chunk in enumerate(chunks):
        mode = "held" if i else "load"
        weights = held if mode == "held" else [gate_weight, up_weight]
        keep, send, *loaded = project(sources, order, meta, weights, chunk, span, rows, mode)
        held = loaded or held
        other = lax.ppermute(send, "row", partner)
        piece = keep.shape[1] // chips
        added = [
            keep[:, s * piece : (s + 1) * piece] + other[:, s * piece : (s + 1) * piece]
            for s in range(chips)
        ]
        values = added[0]
        for s in range(1, chips):
            part = (added[s] * scale).astype(jnp.float16)
            got = lax.ppermute(part, "row", chip_shift(s))
            values = values + got.astype(jnp.float32) * (1 / scale)
        own = (jax.nn.silu(values[0]) * values[1]).astype(jnp.bfloat16)
        mine = [own]
        for s in range(1, chips):
            mine.append(lax.ppermute(own, "row", chip_shift(s)))
        mine = jnp.concatenate(mine, axis=0)
        theirs = lax.ppermute(mine, "row", partner)
        hidden.append(jnp.concatenate([mine, theirs], axis=0))

    def travel(value, lines):
        result = []
        for hop in range(1, cols):
            pairs = [
                (at * cols + r // per_column + hop - 1, at * cols + r // per_column + hop)
                for r, at in lines
                if r // per_column + hop < cols
            ]
            if not pairs:
                break
            value = lax.ppermute(value, ("row", "col"), pairs)
            result.append((value, [(a // cols, a % cols) for _, a in pairs]))
        return result

    def row_choices(value, i):
        split, last = i == split_chunk, i == len(chunks) - 1
        if split:
            classes = {"direct": [("from", lane)]}
        elif last:
            classes = {
                "even": [("below", lane), ("parity", 0)],
                "odd": [("below", lane), ("parity", 1)],
                "late": [("from", lane)],
            }
        elif i > 1:
            classes = {"direct": [("below", lane)], "late": [("from", lane)]}
        else:
            classes = {"direct": []}
        choices = [(value, 0, [], 0)]
        for sources in classes.values():
            lines = [(r, r) for r in range(rows) if all(holds(r // per_column, *c) for c in sources)]
            for hop, (moved, _) in enumerate(travel(value, lines), 1):
                choices.append((moved, hop, sources, 0))
        if split:
            lines = [
                (r, (r + ahead * PAIR) % rows) for r in range(rows) if r // per_column < lane
            ]
            for hop, (moved, ends) in enumerate(travel(value, lines), 1):
                back = [(a * cols + c, (a - ahead * PAIR) % rows * cols + c) for a, c in ends]
                moved = lax.ppermute(moved, ("row", "col"), back)
                choices.append((moved, hop, [("below", lane)], ahead))
        return choices

    can_split = ahead > 0 and ahead * PAIR % per_column == 0 and groups > 3
    split_chunk = 1 if can_split else None
    row_side = []
    if per_column == 1:
        for i, (turns, offset, columns) in enumerate(chunks):
            row_side.append((row_choices(hidden[i], i), turns, offset, columns))
        heights = [(p * part_width, part_width) for p in range(PARTS)]
    else:
        offset = lax.rem(here[0], jnp.int32(per_column)) * own_units
        joined = hidden[: groups - 2] + [jnp.concatenate(hidden[groups - 2 :], axis=1)]
        for i, value in enumerate(joined):
            value = lax.dynamic_slice_in_dim(value, offset, own_units, 1)
            row_side.append((row_choices(value, i), chunks[i][0], 0, own_units))
        heights = [(0, own_units)]

    col_pieces = [
        ([(hidden[i], None, [], 0)], turns, 0, columns, offset)
        for i, (turns, offset, columns) in enumerate(chunks)
    ]
    sizes = (groups, span * shard_rows, rows, per_column)
    columns = collect(col_pieces, (groups * span * shard_rows, width), meta, *sizes)
    out = None
    for start, height in heights:
        row_pieces = [
            (choices, turns, start - offset, height, 0)
            for choices, turns, offset, units in row_side
            if offset <= start and start + height <= offset + units
        ]
        out = gram_rows(row_pieces, columns, out, start, height, (own_units, width), meta, *sizes)
    return out


def solution(mesh):
    mapped = jax.shard_map(
        body,
        mesh=mesh,
        in_specs=(P(("group", "col"), "row"), P("row", "col"), P("row", "col")),
        out_specs=P(("group", "row"), "col"),
        check_vma=False,
    )
    if mesh.shape["row"] == mesh.shape["col"] == 2 * PAIR:
        return mapped
    return mapped
```

```python
import math

import jax
import jax.numpy as jnp
from jax import lax
from jax.experimental import pallas as pl
from jax.experimental.pallas import tpu as pltpu
from jax.sharding import PartitionSpec as P


BLOCK = 1792
TOKEN_MAX = 6.0
WEIGHT_MAX = 0.0625
PAIR = 2
PARTS = 2
MIN_ROWS = 16
AHEAD = 2
PROJECT_VMEM = 18 * 2**20
GRAM_VMEM = 24 * 2**20


def send_scale(features):
    bound = TOKEN_MAX * WEIGHT_MAX * features
    return 2.0 ** math.floor(math.log2(float(jnp.finfo(jnp.float16).max) / bound))


def in_hbm(array):
    return pltpu.with_memory_space_constraint(array, pltpu.HBM)


def holds(column, kind, number):
    if kind == "parity":
        return column % 2 == number
    return column < number if kind == "below" else column >= number


def divisor(limit, *sizes):
    return max(d for d in range(128, limit + 1, 128) if all(s % d == 0 for s in sizes))


def arrival_order(cols, span):
    def distance(c, g):
        return max(abs(g * span + i - c) for i in range(span))

    return [
        sorted(range(cols // span), key=lambda g: (distance(c, g), abs(2 * g * span - cols)))
        for c in range(cols)
    ]


def project(sources, order, meta, weights, chunk, span, rows, mode):
    turns, offset, width = chunk
    count = len(weights)
    cols, groups = len(order), len(order[0])
    shard_rows, features = sources[0].shape
    options = [
        sorted({order[c][k] * span + i - c for c in range(cols)}) for k in turns for i in range(span)
    ]
    used = sorted(set().union(*options))
    tokens = len(options) * shard_rows
    piece = tokens // rows
    chips = rows // PAIR
    half = tokens // PAIR
    per_shard = shard_rows // piece
    tile = divisor(512, width) if width % 512 == 0 else divisor(896, width)
    steps = width // tile

    def kernel(meta, *refs):
        source_refs = dict(zip(used, refs[: len(used)]))
        given, keep_ref, send_ref = refs[len(used) :][:count], *refs[len(used) + count :][:2]
        if mode == "load":
            weight_refs = refs[len(used) + count + 2 :][:count]
            held, sems, load_sems = refs[-3:]
        else:
            weight_refs = given
            held, sems = refs[-2:]

        def load_copy(index, j):
            block = pl.ds(pl.multiple_of(offset + j * tile, 128), tile)
            source, target = given[index].at[:, block], weight_refs[index].at[:, block]
            return pltpu.make_async_copy(source, target, load_sems.at[index, j])

        @pl.when(pl.program_id(0) == 0)
        def _():
            chip, core, col = meta[0] // PAIR, lax.rem(meta[0], PAIR), meta[1]
            waits = []
            for i, distances in enumerate(options):
                group = meta[2 + col * groups + turns[i // span]]
                away = group * span + i % span - col
                for b in range(per_shard):
                    q = i * per_shard + b
                    step = lax.rem(q // PAIR - chip + chips, chips)
                    role = jnp.where(core == q % PAIR, 0, chips) + step
                    target = held.at[pl.ds(pl.multiple_of(role * piece, piece), piece)]
                    for d in distances:
                        copy = pltpu.make_async_copy(
                            source_refs[d].at[pl.ds(b * piece, piece)], target, sems.at[q]
                        )
                        pl.when(away == d)(copy.start)
                    waits.append(
                        pltpu.make_async_copy(
                            source_refs[distances[0]].at[pl.ds(b * piece, piece)], target, sems.at[q]
                        )
                    )
            if mode != "held":
                for j in range(min(AHEAD, steps)):
                    for index in range(count):
                        load_copy(index, j).start()
            for wait in waits:
                wait.wait()

        if mode != "held":

            @pl.when(pl.program_id(0) + AHEAD < steps)
            def _():
                for index in range(count):
                    load_copy(index, pl.program_id(0) + AHEAD).start()

        here = pl.ds(pl.multiple_of(offset + pl.program_id(0) * tile, 128), tile)
        for index, weight in enumerate(weight_refs):
            if mode != "held":
                load_copy(index, pl.program_id(0)).wait()
            result = jnp.dot(held[...], weight[:, here], preferred_element_type=jnp.float32)
            keep_ref[index] = result[:half]
            send_ref[index] = result[half:]

    vmem_spec = pl.BlockSpec(memory_space=pltpu.VMEM)
    hbm_spec = pl.BlockSpec(memory_space=pltpu.HBM)
    weight_spec = vmem_spec if mode == "held" else hbm_spec
    out_spec = pl.BlockSpec((count, half, tile), lambda j, meta: (0, 0, j))
    return pl.pallas_call(
        kernel,
        grid_spec=pltpu.PrefetchScalarGridSpec(
            num_scalar_prefetch=1,
            grid=(steps,),
            in_specs=[hbm_spec] * len(used) + [weight_spec] * count,
            out_specs=[out_spec] * 2 + [vmem_spec] * (count if mode == "load" else 0),
            scratch_shapes=[
                pltpu.VMEM((tokens, features), sources[0].dtype),
                pltpu.SemaphoreType.DMA((rows,)),
            ]
            + ([] if mode == "held" else [pltpu.SemaphoreType.DMA((count, steps))]),
        ),
        out_shape=[pltpu.HBM((count, half, width), jnp.float32)] * 2
        + ([pltpu.VMEM(w.shape, w.dtype) for w in weights] if mode == "load" else []),
        cost_estimate=pl.CostEstimate(
            flops=2 * count * tokens * features * width,
            bytes_accessed=2 * count * (features + 4 * half) * width,
            transcendentals=0,
        ),
        compiler_params=pltpu.CompilerParams(vmem_limit_bytes=PROJECT_VMEM),
    )(meta, *[in_hbm(sources[d]) for d in used], *(weights if mode == "held" else map(in_hbm, weights)))


def placed(pieces, groups, group_rows, rows, per_column, of_row):
    chips = rows // PAIR
    arrays = []

    def index_of(array):
        for i, other in enumerate(arrays):
            if other is array:
                return i
        arrays.append(array)
        return len(arrays) - 1

    plan = []
    for choices, turns, source_column, columns, column in pieces:
        indexed = [(index_of(a), *rest) for a, *rest in choices]
        plan += [(indexed, turns, b, source_column, columns, column) for b in range(rows)]

    def run(meta, array_refs, held, sems):
        row, col = meta[0], meta[1]
        chip, core, source = row // PAIR, lax.rem(row, PAIR), row // per_column
        hop = col - source
        waits = []
        for n, (choices, turns, b, source_column, columns, column) in enumerate(plan):
            piece = len(turns) * group_rows // rows
            for index, distance, sources, ahead in choices:
                chip_b = lax.rem(chip + ahead - b % chips + chips, chips)
                core_b = lax.rem(core + b // chips, PAIR)
                place = (chip_b * PAIR + core_b) * piece
                slot = turns[0] + place // group_rows
                position = meta[2 + (source if of_row else col) * groups + slot]
                target_row = position * group_rows + lax.rem(place, group_rows)
                copy = pltpu.make_async_copy(
                    array_refs[index].at[pl.ds(b * piece, piece), pl.ds(source_column, columns)],
                    held.at[pl.ds(pl.multiple_of(target_row, piece), piece), pl.ds(column, columns)],
                    sems.at[n],
                )
                chosen = jnp.bool_(True)
                if distance is not None:
                    chosen = jnp.maximum(hop, 0) == distance
                for condition in sources:
                    chosen = chosen & holds(source, *condition)
                pl.when(chosen)(copy.start)
            waits.append(copy)
        for wait in waits:
            wait.wait()

    return arrays, len(plan), run


def collect(pieces, shape, meta, groups, group_rows, rows, per_column):
    arrays, copies, run = placed(pieces, groups, group_rows, rows, per_column, False)

    def kernel(meta, *refs):
        run(meta, refs[: len(arrays)], refs[-2], refs[-1])

    return pl.pallas_call(
        kernel,
        grid_spec=pltpu.PrefetchScalarGridSpec(
            num_scalar_prefetch=1,
            grid=(1,),
            in_specs=[pl.BlockSpec(memory_space=pl.ANY)] * len(arrays),
            out_specs=pl.BlockSpec(memory_space=pltpu.VMEM),
            scratch_shapes=[pltpu.SemaphoreType.DMA((copies,))],
        ),
        out_shape=pltpu.VMEM(shape, arrays[0].dtype),
        compiler_params=pltpu.CompilerParams(vmem_limit_bytes=GRAM_VMEM),
        name="collect",
    )(meta, *arrays)


def gram_rows(row_pieces, columns, out, start, height, shape, meta, groups, group_rows, rows, per_column):
    width = shape[1]
    tile = divisor(256, height, start, BLOCK) if start else divisor(256, height, BLOCK)
    segment = divisor(1792, width, BLOCK)
    tokens = groups * group_rows
    arrays, copies, run = placed(row_pieces, groups, group_rows, rows, per_column, True)

    def kernel(meta, *refs):
        columns_ref = refs[len(arrays)]
        out_ref, row_held, sems = refs[-3:]
        row, col = meta[0], meta[1]

        @pl.when(pl.program_id(0) == 0)
        def _():
            run(meta, refs[: len(arrays)], row_held, sems)

        own_units = shape[0]
        i = pl.program_id(0)
        row_block = (row * own_units + start + i * tile) // BLOCK
        for j in range(0, width, segment):
            col_block = (col * width + j) // BLOCK

            @pl.when(row_block <= col_block)
            def _():
                a = row_held[:, pl.ds(pl.multiple_of(i * tile, tile), tile)]
                total = lax.dot_general(
                    a,
                    columns_ref[:, j : j + segment],
                    (((0,), (0,)), ((), ())),
                    preferred_element_type=jnp.float32,
                )
                out_ref[:, j : j + segment] = total * (2.0 / tokens)

            @pl.when(row_block > col_block)
            def _():
                out_ref[:, j : j + segment] = jnp.zeros((tile, segment), jnp.float32)

    in_specs = [pl.BlockSpec(memory_space=pl.ANY)] * len(arrays)
    in_specs.append(pl.BlockSpec(memory_space=pltpu.VMEM))
    args = [*arrays, columns]
    aliases = {}
    if out is not None:
        in_specs.append(pl.BlockSpec(memory_space=pl.ANY))
        aliases = {1 + len(args): 0}
        args.append(out)
    first = start // tile
    return pl.pallas_call(
        kernel,
        grid_spec=pltpu.PrefetchScalarGridSpec(
            num_scalar_prefetch=1,
            grid=(height // tile,),
            in_specs=in_specs,
            out_specs=pl.BlockSpec((tile, width), lambda i, meta: (first + i, 0)),
            scratch_shapes=[
                pltpu.VMEM((tokens, height), columns.dtype),
                pltpu.SemaphoreType.DMA((copies,)),
            ],
        ),
        out_shape=jax.ShapeDtypeStruct(shape, jnp.float32),
        input_output_aliases=aliases,
        cost_estimate=pl.CostEstimate(
            flops=2 * tokens * height * width, bytes_accessed=4 * height * width, transcendentals=0
        ),
        compiler_params=pltpu.CompilerParams(vmem_limit_bytes=GRAM_VMEM),
    )(meta, *args)


def body(tokens, gate_weight, up_weight):
    rows = lax.axis_size("row")
    cols = lax.axis_size("col")
    chips = rows // PAIR
    shard_rows, features = tokens.shape
    width = gate_weight.shape[1]
    per_column = rows // cols
    own_units = width // per_column
    span = max(1, MIN_ROWS * rows // shard_rows)
    groups = cols // span
    order = arrival_order(cols, span)
    scale = send_scale(features * PAIR)
    lane = cols // 2
    ahead = chips // 2

    here = jnp.stack([lax.axis_index("row"), lax.axis_index("col")]).astype(jnp.int32)
    table = jnp.array([g for c in order for g in c], jnp.int32)
    meta = jnp.concatenate([here, table])

    partner = [(r, r ^ 1) for r in range(rows)]

    def chip_shift(s):
        return [(r, (r + s * PAIR) % rows) for r in range(rows)]

    sources = {0: tokens}
    right = left = tokens
    for d in range(1, cols):
        right = lax.ppermute(right, "col", [(c, c + 1) for c in range(d - 1, cols - 1)])
        left = lax.ppermute(left, "col", [(c, c - 1) for c in range(1, cols - d + 1)])
        sources[-d], sources[d] = right, left

    part_width = width // PARTS
    chunks = [([k], 0, width) for k in range(groups - 2)]
    chunks += [([groups - 2, groups - 1], p * part_width, part_width) for p in range(PARTS)]

    hidden = []
    held = []
    for i, chunk in enumerate(chunks):
        mode = "held" if i else "load"
        weights = held if mode == "held" else [gate_weight, up_weight]
        keep, send, *loaded = project(sources, order, meta, weights, chunk, span, rows, mode)
        held = loaded or held
        other = lax.ppermute(send, "row", partner)
        piece = keep.shape[1] // chips
        got = []
        for s in range(1, chips):
            away = slice(s * piece, (s + 1) * piece)
            part = ((keep[:, away] + other[:, away]) * scale).astype(jnp.float16)
            got.append(lax.ppermute(part, "row", chip_shift(s)))
        gate_values, up_values = (
            sum((g[n].astype(jnp.float32) * (1 / scale) for g in got),
                keep[n, :piece] + other[n, :piece])
            for n in range(2)
        )
        own = (jax.nn.silu(gate_values) * up_values).astype(jnp.bfloat16)
        mine = [own]
        for s in range(1, chips):
            mine.append(lax.ppermute(own, "row", chip_shift(s)))
        mine = jnp.concatenate(mine, axis=0)
        theirs = lax.ppermute(mine, "row", partner)
        hidden.append(jnp.concatenate([mine, theirs], axis=0))

    def travel(value, lines):
        result = []
        for hop in range(1, cols):
            pairs = [
                (at * cols + r // per_column + hop - 1, at * cols + r // per_column + hop)
                for r, at in lines
                if r // per_column + hop < cols
            ]
            if not pairs:
                break
            value = lax.ppermute(value, ("row", "col"), pairs)
            result.append((value, [(a // cols, a % cols) for _, a in pairs]))
        return result

    def row_choices(value, i):
        split, last = i == split_chunk, i == len(chunks) - 1
        if split:
            classes = {"d": [("from", lane)]}
        elif last:
            classes = {
                "e": [("below", lane), ("parity", 0)],
                "o": [("below", lane), ("parity", 1)],
                "t": [("from", lane)],
            }
        elif i > 1:
            classes = {"d": [("below", lane)], "t": [("from", lane)]}
        else:
            classes = {"d": []}
        choices = [(value, 0, [], 0)]
        for sources in classes.values():
            lines = [(r, r) for r in range(rows) if all(holds(r // per_column, *c) for c in sources)]
            for hop, (moved, _) in enumerate(travel(value, lines), 1):
                choices.append((moved, hop, sources, 0))
        if split:
            lines = [
                (r, (r + ahead * PAIR) % rows) for r in range(rows) if r // per_column < lane
            ]
            for hop, (moved, ends) in enumerate(travel(value, lines), 1):
                back = [(a * cols + c, (a - ahead * PAIR) % rows * cols + c) for a, c in ends]
                moved = lax.ppermute(moved, ("row", "col"), back)
                choices.append((moved, hop, [("below", lane)], ahead))
        return choices

    can_split = ahead > 0 and ahead * PAIR % per_column == 0 and groups > 3
    split_chunk = 1 if can_split else None
    row_side = []
    if per_column == 1:
        for i, (turns, offset, columns) in enumerate(chunks):
            row_side.append((row_choices(hidden[i], i), turns, offset, columns))
        heights = [(p * part_width, part_width) for p in range(PARTS)]
    else:
        offset = lax.rem(here[0], jnp.int32(per_column)) * own_units
        joined = hidden[: groups - 2] + [jnp.concatenate(hidden[groups - 2 :], axis=1)]
        for i, value in enumerate(joined):
            value = lax.dynamic_slice_in_dim(value, offset, own_units, 1)
            row_side.append((row_choices(value, i), chunks[i][0], 0, own_units))
        heights = [(0, own_units)]

    col_pieces = [
        ([(hidden[i], None, [], 0)], turns, 0, columns, offset)
        for i, (turns, offset, columns) in enumerate(chunks)
    ]
    sizes = (groups, span * shard_rows, rows, per_column)
    columns = collect(col_pieces, (groups * span * shard_rows, width), meta, *sizes)
    out = None
    for start, height in heights:
        row_pieces = [
            (choices, turns, start - offset, height, 0)
            for choices, turns, offset, units in row_side
            if offset <= start and start + height <= offset + units
        ]
        out = gram_rows(row_pieces, columns, out, start, height, (own_units, width), meta, *sizes)
    return out


def solution(mesh):
    mapped = jax.shard_map(
        body,
        mesh=mesh,
        in_specs=(P(("group", "col"), "row"), P("row", "col"), P("row", "col")),
        out_specs=P(("group", "row"), "col"),
        check_vma=False,
    )
    if mesh.shape["row"] == mesh.shape["col"] == 2 * PAIR:
        return mapped
    return mapped
```
